256 devices in a mesh: replica: 8 (over x_hi, y), shard: 32 (over z, x_lo, core).
Axes of the slice: x: 4 (x_hi: 2, x_lo: 2; x = x_hi * 2 + x_lo), y: 4, z: 8, core: 2. Of those that a mesh axis runs over, the one named last changes fastest.
Arguments:
- master_weight: float32 [32, 1024, 4096], P(None, 'replica', 'shard'), may hold values from -0.1875 to 0.1875
- gradient: bfloat16 [32, 1024, 4096], P(None, 'replica', 'shard'), may hold values from -6 to 6
- first_moment: bfloat16 [32, 1024, 4096], P(None, 'replica', 'shard'), may hold values from -1.796875 to 1.796875
- second_moment: bfloat16 [32, 1024, 4096], P(None, 'replica', 'shard'), may hold values from 0.049804688 to 2
- hidden: bfloat16 [8, 32, 384, 1024], P('replica', 'shard'), may hold values from -6 to 6
- owner_of_expert: int32 [32], replicated, may hold values from 0 to 31, each once
- slab_order: int32 [8], replicated, may hold values from 0 to 7, each once
Outputs:
- new_master: float32 [32, 1024, 4096], P(None, 'replica', 'shard')
- new_first: bfloat16 [32, 1024, 4096], P(None, 'replica', 'shard')
- new_second: bfloat16 [32, 1024, 4096], P(None, 'replica', 'shard')
- expert_out: bfloat16 [8, 32, 384, 4096], P('replica', 'shard')
The draws below stay inside these ranges and needn't reach their ends.
Inputs may be any that keep to these rules, and one draw needn't show every extreme that they name: `owner_of_expert`: a permutation: every owner holds exactly one expert. A permutation: row slab j of the learner's arrays holds hidden units from slab_order[j] * 128 on.
All inputs are finite; a program needn't handle non-finite values.
Results may differ from the reference program's by a relative error of at most 0.0049.
Values may be sent and summed in bfloat16 or wider, within the bound.
A program may use at most 128 MiB of HBM per device.

```python
import math
import jax
import jax.numpy as jnp
from jax import lax

D = 4096
FFW = 1024
QB = 128
TOK_DEV = 384
EXPERTS = 32
REPLICAS = 8


def block_levels(stream_key, shape, pieces, least, high):
    gain, own = 1.0, jax.random.fold_in(stream_key, 6)
    for axis_at, shards_of in pieces:
        steps = jnp.exp(jax.random.uniform(jax.random.fold_in(own, axis_at), (shards_of,), jnp.float32, least / len(pieces), high / len(pieces)))
        gain = gain * jnp.repeat(steps, shape[axis_at] // shards_of).reshape([-1 if axis == axis_at else 1 for axis in range(len(shape))])
    return gain


def gaussian(key, dims, spread, most, shards=(), held_as=jnp.bfloat16):
    factor_of = block_levels(key, dims, shards, -0.22, 0.18) if shards else 1.0
    array = jax.random.normal(key, dims, jnp.float32) * spread * factor_of
    return jnp.minimum(jnp.maximum(array, -most), most).astype(held_as)


def setup_inputs(seed: int = 0) -> dict:
    arg_keys = jax.random.split(jax.random.key(seed), 8)
    return {
        "master_weight": gaussian(arg_keys[0], (EXPERTS, FFW, D), FFW ** -0.5, 0.1875, ((1, 8), (2, 32)), jnp.float32),
        "gradient": gaussian(arg_keys[1], (EXPERTS, FFW, D), 1.0, 6.0, ((1, 8), (2, 32))),
        "first_moment": gaussian(arg_keys[2], (EXPERTS, FFW, D), 0.3, 1.796875, ((1, 8), (2, 32))),
        "second_moment": jnp.clip(jnp.exp(math.log(2.0) - 3.6927934 * jax.random.uniform(arg_keys[3], (EXPERTS, FFW, D), jnp.float32) ** block_levels(arg_keys[3], (EXPERTS, FFW, D), ((1, 8), (2, 32)), -0.2, 0.2)), 0.049804688, 2.0).astype(jnp.bfloat16),
        "hidden": gaussian(arg_keys[4], (REPLICAS, EXPERTS, TOK_DEV, FFW), 1.0, 6.0, ((0, 8), (1, 32))),
        "owner_of_expert": jax.random.permutation(arg_keys[5], EXPERTS).astype(jnp.int32),
        "slab_order": jax.random.permutation(arg_keys[6], REPLICAS).astype(jnp.int32),
    }


beta_one = 0.9
beta_two = 0.95
learn_rate = 0.004
adam_epsilon = 1e-08
step_count = 10.0
quant_limit = 448.0
scale_epsilon = 1e-06

def adam_step(master_weight, gradient, first_moment, second_moment):
    float_gradient = gradient.astype(jnp.float32)
    moment_one = beta_one * first_moment.astype(jnp.float32) + (1.0 - beta_one) * float_gradient
    moment_two = beta_two * second_moment.astype(jnp.float32) + (1.0 - beta_two) * float_gradient * float_gradient
    first_fix = 1.0 - beta_one ** step_count
    second_fix = 1.0 - beta_two ** step_count
    update = moment_one / first_fix / (jnp.sqrt(moment_two / second_fix) + adam_epsilon)
    return (master_weight - learn_rate * update, moment_one, moment_two)

def quantize(weights):
    number, height, breadth = weights.shape
    blocks = weights.reshape(number, height // QB, QB, breadth // QB, QB)
    largest = lax.optimization_barrier(jnp.max(jnp.abs(blocks), axis=(2, 4)))
    block_scale = ((largest + scale_epsilon) / quant_limit).astype(jnp.bfloat16)
    block_scale = lax.optimization_barrier(block_scale)
    divided = blocks / block_scale.astype(jnp.float32)[:, :, None, :, None]
    return (divided.astype(jnp.bfloat16).reshape(number, height, breadth), block_scale)

def scaled_product(summed, left_part, quant_rows, scale_rows):
    token_count = left_part.shape[0]
    breadth = quant_rows.shape[1]
    for row_block in range(scale_rows.shape[0]):
        partial_value = jnp.dot(left_part[:, row_block * QB:(row_block + 1) * QB], quant_rows[row_block * QB:(row_block + 1) * QB], preferred_element_type=jnp.float32)
        factor = scale_rows[row_block].astype(jnp.float32)
        summed = summed + (partial_value.reshape(token_count, breadth // QB, QB) * factor[None, :, None]).reshape(token_count, breadth)
    return summed

def reference(master_weight, gradient, first_moment, second_moment, hidden, owner_of_expert, slab_order):
    updated, moment_one, moment_two = adam_step(master_weight, gradient, first_moment, second_moment)
    quantized, block_scale = quantize(updated)
    experts = quantized.shape[0]
    replicas = slab_order.shape[0]
    unit_count = quantized.shape[1]
    slab_rows = unit_count // replicas
    tokens = hidden.shape[2]
    places = jnp.arange(experts, dtype=jnp.int32)
    held_expert = lax.optimization_barrier(jnp.sum(jnp.where(owner_of_expert[None, :] == places[:, None], places[None, :], 0), axis=1)).astype(jnp.int32)
    ordered = hidden.reshape(replicas, experts, tokens, replicas, slab_rows)[:, :, :, slab_order, :]
    ordered = ordered.reshape(replicas, experts, tokens, unit_count)

    def one_owner(owner_index):
        expert = held_expert[owner_index]
        expert_quant = quantized[expert]
        expert_scale = block_scale[expert]
        left_part = ordered[:, owner_index].reshape(replicas * tokens, unit_count)
        zero_sum = jnp.zeros((replicas * tokens, expert_quant.shape[1]), jnp.float32)
        return scaled_product(zero_sum, left_part, expert_quant, expert_scale).astype(jnp.bfloat16)
    results = lax.map(one_owner, places)
    expert_out = results.reshape(experts, replicas, tokens, results.shape[-1]).transpose(1, 0, 2, 3)
    return (updated, moment_one.astype(jnp.bfloat16), moment_two.astype(jnp.bfloat16), expert_out)
```

```python
import functools

import jax
import jax.numpy as jnp
from jax import lax
from jax.experimental import pallas as pl
from jax.experimental.pallas import tpu as pltpu
from jax.sharding import PartitionSpec as P

D = 4096
FFW = 1024
QB = 128
TOK = 384
EXPERTS = 32
REPLICAS = 8
ZS = 8
GROUP = 4

beta_one = 0.9
beta_two = 0.95
learn_rate = 0.004
adam_epsilon = 1e-08
step_count = 10.0
quant_limit = 448.0
scale_epsilon = 1e-06
first_fix = 1.0 - beta_one**step_count
second_fix = 1.0 - beta_two**step_count

MESH = pl.DeviceIdType.MESH
ADAM_STEP = 8


def adam_kernel(
    owner_ref, slab_ref, w_ref, g_ref, m_ref, v_ref, ha_ref, hb_ref, nw_ref, nm_ref, nv_ref, out_ref, ho_ref
):
    step = pl.program_id(0)
    ho_ref[:, :QB] = ha_ref[...]
    ho_ref[:, QB:] = hb_ref[...]
    for i in range(ADAM_STEP):
        g = g_ref[i].astype(jnp.float32)
        first = beta_one * m_ref[i].astype(jnp.float32) + (1.0 - beta_one) * g
        second = beta_two * v_ref[i].astype(jnp.float32) + (1.0 - beta_two) * g * g
        update = first / first_fix / (jnp.sqrt(second / second_fix) + adam_epsilon)
        w = w_ref[i] - learn_rate * update
        nw_ref[i] = w
        nm_ref[i] = first.astype(jnp.bfloat16)
        nv_ref[i] = second.astype(jnp.bfloat16)
        largest = jnp.max(jnp.abs(w), axis=(0, 1), keepdims=True)
        scale = ((largest + scale_epsilon) / quant_limit).astype(jnp.bfloat16).astype(jnp.float32)
        quantized = (w * (1.0 / scale)).astype(jnp.bfloat16).astype(jnp.float32)
        out_ref[owner_ref[step * ADAM_STEP + i]] = (quantized * scale).astype(jnp.bfloat16)


def adam(owner, slab, w, g, m, v, hidden):
    block = pl.BlockSpec((ADAM_STEP, QB, QB), lambda e, o, p: (e, 0, 0))
    whole = pl.BlockSpec((EXPERTS, QB, QB), lambda e, o, p: (0, 0, 0))
    even = pl.BlockSpec((TOK, QB), lambda e, o, p: (0, p[2 * e]))
    odd = pl.BlockSpec((TOK, QB), lambda e, o, p: (0, p[2 * e + 1]))
    pair = pl.BlockSpec((TOK, 2 * QB), lambda e, o, p: (0, e))
    shape = (EXPERTS, QB, QB)
    return pl.pallas_call(
        adam_kernel,
        out_shape=(
            jax.ShapeDtypeStruct(shape, jnp.float32),
            jax.ShapeDtypeStruct(shape, jnp.bfloat16),
            jax.ShapeDtypeStruct(shape, jnp.bfloat16),
            jax.ShapeDtypeStruct(shape, jnp.bfloat16),
            jax.ShapeDtypeStruct((TOK, FFW), jnp.bfloat16),
        ),
        grid_spec=pltpu.PrefetchScalarGridSpec(
            num_scalar_prefetch=2,
            grid=(EXPERTS // ADAM_STEP,),
            in_specs=[block] * 4 + [even, odd],
            out_specs=(block, block, block, whole, pair),
        ),
        compiler_params=pltpu.CompilerParams(
            dimension_semantics=("arbitrary",), vmem_limit_bytes=24 * 2**20
        ),
        name="adam_quantize",
    )(owner, slab, w, g, m, v, hidden, hidden)


ORDER = (0, 1, 7, 2, 6, 3, 5, 4)
SPLIT = ((3, 2, 0), (2, 1, 1), (3, 1, 1), (2, 1, 1)) * 2


def deliver_kernel(mine, ordered, out, full, obuf, asem, ssem, rsem, osem, lsem):
    r, s = lax.axis_index("replica"), lax.axis_index("shard")
    xh, y = r // 4, r % 4
    z, xl, c = s // 4, (s // 2) % 2, s % 2
    xo = 1 - xh
    up, down, far = (y + 1) % 4, (y + 3) % 4, (y + 2) % 4

    def peer(dz, dx, dc):
        return ((z + dz) % ZS) * 4 + ((xl + dx) % 2) * 2 + (c + dc) % 2

    others = [(dx, dc) for dx in range(2) for dc in range(2)]
    exchange = [(i, dx, dc) for i in range(ZS) for dx, dc in others if (ORDER[i], dx, dc) != (0, 0, 0)]

    barrier = pltpu.get_barrier_semaphore()
    for i, dx, dc in exchange:
        pl.semaphore_signal(barrier, inc=1, device_id=(r, peer(ORDER[i], dx, dc)), device_id_type=MESH)
    for there in ((xh * 4 + up, s), (xh * 4 + down, s), (xo * 4 + y, s)):
        pl.semaphore_signal(barrier, inc=1, device_id=there, device_id_type=MESH)
    pl.semaphore_wait(barrier, len(exchange) + 3)

    own = pltpu.make_async_copy(mine.at[s], full.at[r, s], lsem)
    own.start()
    first = []
    for n, (i, dx, dc) in enumerate(exchange):
        p = peer(ORDER[i], dx, dc)
        copy = pltpu.make_async_remote_copy(
            mine.at[p], full.at[r, s], asem.at[0, n], asem.at[1, n], device_id=(r, p), device_id_type=MESH
        )
        copy.start()
        first.append(copy)

    pending = []
    serial = {}

    def send(group, kind, row, begin, count, there):
        at = serial.setdefault((group, kind), len(serial))
        tiles = full.at[row, pl.ds(begin, count)]
        copy = pltpu.make_async_remote_copy(
            tiles, tiles, ssem.at[at], rsem.at[at], device_id=there, device_id_type=MESH
        )
        copy.start()
        pending.append(copy)

    def arrive(group, kind, row, begin, count):
        at = serial[(group, kind)]
        tiles = full.at[row, pl.ds(begin, count)]
        pltpu.make_async_remote_copy(
            tiles, tiles, ssem.at[at], rsem.at[at], device_id=(r, s), device_id_type=MESH
        ).wait_recv()

    def base_of(i):
        return ((z + ORDER[i]) % ZS) * GROUP

    def at_row(hi, yy):
        return hi * 4 + yy

    to_up, to_down, to_x = (xh * 4 + up, s), (xh * 4 + down, s), (xo * 4 + y, s)

    def stage0(i):
        base = base_of(i)
        if i == 0:
            own.wait()
        for n, (k, dx, dc) in enumerate(exchange):
            if k == i:
                src = peer(ORDER[i], dx, dc)
                pltpu.make_async_remote_copy(
                    mine.at[0], full.at[r, src], asem.at[0, n], asem.at[1, recv_slot(n)], device_id=(r, s),
                    device_id_type=MESH,
                ).wait_recv()
        np_, hp, hq = SPLIT[i]
        nq = GROUP - np_
        send(i, "px", r, base, np_, to_x)
        send(i, "py+", r, base, np_, to_up)
        send(i, "py-", r, base, np_, to_down)
        send(i, "qy+", r, base + np_, nq, to_up)
        send(i, "qy-", r, base + np_, nq, to_down)
        send(i, "qx0", r, base + np_, nq, to_x)

    def recv_slot(n):
        i, dx, dc = exchange[n]
        mirrored = (ORDER.index((ZS - ORDER[i]) % ZS), dx, dc)
        return exchange.index(mirrored)

    def stage1(i):
        base = base_of(i)
        np_, hp, hq = SPLIT[i]
        nq = GROUP - np_
        qb = base + np_
        arrive(i, "px", at_row(xo, y), base, np_)
        send(i, "xy+", at_row(xo, y), base, np_, to_up)
        send(i, "xy-", at_row(xo, y), base, np_, to_down)
        arrive(i, "py+", at_row(xh, down), base, np_)
        send(i, "pf+", at_row(xh, down), base, hp, to_up)
        arrive(i, "py-", at_row(xh, up), base, np_)
        send(i, "pf-", at_row(xh, up), base + hp, np_ - hp, to_down)
        arrive(i, "qy+", at_row(xh, down), qb, nq)
        if hq:
            send(i, "qf+", at_row(xh, down), qb, hq, to_up)
        send(i, "qx1", at_row(xh, down), qb, nq, to_x)
        arrive(i, "qy-", at_row(xh, up), qb, nq)
        if nq - hq:
            send(i, "qf-", at_row(xh, up), qb + hq, nq - hq, to_down)
        send(i, "qx2", at_row(xh, up), qb, nq, to_x)

    def stage2(i):
        base = base_of(i)
        np_, hp, hq = SPLIT[i]
        nq = GROUP - np_
        qb = base + np_
        arrive(i, "xy+", at_row(xo, down), base, np_)
        send(i, "xf+", at_row(xo, down), base, hp, to_up)
        arrive(i, "xy-", at_row(xo, up), base, np_)
        send(i, "xf-", at_row(xo, up), base + hp, np_ - hp, to_down)
        if hq:
            arrive(i, "qf+", at_row(xh, far), qb, hq)
        if nq - hq:
            arrive(i, "qf-", at_row(xh, far), qb + hq, nq - hq)
        send(i, "qx3", at_row(xh, far), qb, nq, to_x)

    writes = [None, None]

    def stage3(i):
        base = base_of(i)
        np_, hp, hq = SPLIT[i]
        nq = GROUP - np_
        qb = base + np_
        arrive(i, "pf+", at_row(xh, far), base, hp)
        arrive(i, "pf-", at_row(xh, far), base + hp, np_ - hp)
        arrive(i, "qx0", at_row(xo, y), qb, nq)
        arrive(i, "qx1", at_row(xo, down), qb, nq)
        arrive(i, "qx2", at_row(xo, up), qb, nq)
        arrive(i, "xf+", at_row(xo, far), base, hp)
        arrive(i, "xf-", at_row(xo, far), base + hp, np_ - hp)
        arrive(i, "qx3", at_row(xo, far), qb, nq)
        slot = i % 2
        if writes[slot] is not None:
            writes[slot].wait()
        for half in range(2):
            right = jnp.concatenate(
                [full[:, base + half * 2 + k].reshape(FFW, QB) for k in range(2)], axis=1
            )
            value = jnp.dot(ordered[...], right, preferred_element_type=jnp.float32)
            obuf[slot, :, half * 2 * QB:(half + 1) * 2 * QB] = value.astype(jnp.bfloat16)
        columns = pl.ds(pl.multiple_of(base * QB, GROUP * QB), GROUP * QB)
        writes[slot] = pltpu.make_async_copy(obuf.at[slot], out.at[:, columns], osem.at[slot])
        writes[slot].start()

    stages = (stage0, stage1, stage2, stage3)
    for t in range(ZS + len(stages) - 1):
        for lag, stage in enumerate(stages):
            if 0 <= t - lag < ZS:
                stage(t - lag)
    for copy in first:
        copy.wait_send()
    for copy in pending:
        copy.wait_send()
    for write in writes:
        write.wait()


def deliver(mine, ordered):
    copies = 17 * ZS
    return pl.pallas_call(
        deliver_kernel,
        out_shape=jax.ShapeDtypeStruct((TOK, D), jnp.bfloat16),
        in_specs=[
            pl.BlockSpec(memory_space=pltpu.VMEM),
            pl.BlockSpec(memory_space=pltpu.VMEM),
        ],
        out_specs=pl.BlockSpec(memory_space=pl.ANY),
        scratch_shapes=[
            pltpu.VMEM((REPLICAS, EXPERTS, QB, QB), jnp.bfloat16),
            pltpu.VMEM((2, TOK, GROUP * QB), jnp.bfloat16),
            pltpu.SemaphoreType.DMA((2, EXPERTS - 1)),
            pltpu.SemaphoreType.DMA((copies,)),
            pltpu.SemaphoreType.DMA((copies,)),
            pltpu.SemaphoreType.DMA((2,)),
            pltpu.SemaphoreType.DMA,
        ],
        compiler_params=pltpu.CompilerParams(
            collective_id=0, has_side_effects=True, vmem_limit_bytes=40 * 2**20
        ),
        name="deliver",
    )(mine, ordered)


def body(master_weight, gradient, first_moment, second_moment, hidden, owner_of_expert, slab_order):
    updated, moment_one, moment_two, outgoing, ordered = adam(
        owner_of_expert, slab_order, master_weight, gradient, first_moment, second_moment, hidden.reshape(TOK, FFW)
    )
    expert_out = deliver(outgoing, ordered)
    return updated, moment_one, moment_two, expert_out.reshape(1, 1, TOK, D)


def solution(mesh):
    learner = P(None, "replica", "shard")
    rollout = P("replica", "shard", None, None)
    return jax.shard_map(
        body,
        mesh=mesh,
        in_specs=(learner, learner, learner, learner, rollout, P(), P()),
        out_specs=(learner, learner, learner, rollout),
        check_vma=False,
    )
```

```python
import functools

import jax
import jax.numpy as jnp
from jax import lax
from jax.experimental import pallas as pl
from jax.experimental.pallas import tpu as pltpu
from jax.sharding import PartitionSpec as P

D = 4096
FFW = 1024
QB = 128
TOK = 384
EXPERTS = 32
REPLICAS = 8
ZS = 8

beta_one = 0.9
beta_two = 0.95
learn_rate = 0.004
adam_epsilon = 1e-08
step_count = 10.0
quant_limit = 448.0
scale_epsilon = 1e-06
first_fix = 1.0 - beta_one**step_count
second_fix = 1.0 - beta_two**step_count

MESH = pl.DeviceIdType.MESH
CHUNK = 4
CHUNKS = EXPERTS // CHUNK


def adam_kernel(
    owner, slab, w_hbm, g_hbm, m_hbm, v_hbm, hidden, nw_hbm, nm_hbm, nv_hbm, mine, ordered,
    w_in, g_in, m_in, v_in, w_out, m_out, v_out, in_sem, out_sem, slab_sem,
):
    def loads(k):
        part = pl.ds(k * CHUNK, CHUNK)
        return [
            pltpu.make_async_copy(hbm.at[part], vmem.at[part], in_sem.at[j, k])
            for j, (hbm, vmem) in enumerate(((g_hbm, g_in), (m_hbm, m_in), (v_hbm, v_in), (w_hbm, w_in)))
        ]

    def stores(k):
        part = pl.ds(k * CHUNK, CHUNK)
        return [
            pltpu.make_async_copy(vmem.at[part], hbm.at[part], out_sem.at[j, k])
            for j, (vmem, hbm) in enumerate(((w_out, nw_hbm), (m_out, nm_hbm), (v_out, nv_hbm)))
        ]

    xh = lax.axis_index("replica") // 4
    xl = (lax.axis_index("shard") // 2) % 2

    def place_of(e):
        to = owner[e]
        return (to // 4) * 4 + (to % 2) * 2 + (to // 2 + xl) % 2

    for k in range(CHUNKS):
        for copy in loads(k):
            copy.start()
    slabs = []
    for j in range(REPLICAS):
        begin = pl.multiple_of(slab[(xh * 4 + j) % REPLICAS] * QB, QB)
        slabs.append(
            pltpu.make_async_copy(hidden.at[:, pl.ds(begin, QB)], ordered.at[:, pl.ds(j * QB, QB)], slab_sem.at[j])
        )
        slabs[j].start()

    @pl.loop(0, CHUNKS)
    def _(k):
        for copy in loads(k):
            copy.wait()
        for i in range(CHUNK):
            e = k * CHUNK + i
            g = g_in[e].astype(jnp.float32)
            first = beta_one * m_in[e].astype(jnp.float32) + (1.0 - beta_one) * g
            second = beta_two * v_in[e].astype(jnp.float32) + (1.0 - beta_two) * g * g
            update = (learn_rate / first_fix) * first / (jnp.sqrt(second * (1.0 / second_fix)) + adam_epsilon)
            w = w_in[e] - update
            w_out[e] = w
            m_out[e] = first.astype(jnp.bfloat16)
            v_out[e] = second.astype(jnp.bfloat16)
            largest = jnp.max(jnp.abs(w), axis=(0, 1), keepdims=True)
            scale = ((largest + scale_epsilon) / quant_limit).astype(jnp.bfloat16).astype(jnp.float32)
            quantized = (w * (1.0 / scale)).astype(jnp.bfloat16).astype(jnp.float32)
            mine[place_of(e)] = (quantized * scale).astype(jnp.bfloat16)
        for copy in stores(k):
            copy.start()

    for copy in slabs:
        copy.wait()
    for k in range(CHUNKS):
        for copy in stores(k):
            copy.wait()


def adam(owner, slab, w, g, m, v, hidden):
    shape = (EXPERTS, QB, QB)
    hbm = pl.BlockSpec(memory_space=pltpu.HBM)
    smem = pl.BlockSpec(memory_space=pltpu.SMEM)
    vmem = pl.BlockSpec(memory_space=pltpu.VMEM)
    f32, bf16 = jnp.float32, jnp.bfloat16
    return pl.pallas_call(
        adam_kernel,
        out_shape=(
            jax.ShapeDtypeStruct(shape, f32),
            jax.ShapeDtypeStruct(shape, bf16),
            jax.ShapeDtypeStruct(shape, bf16),
            jax.ShapeDtypeStruct(shape, bf16),
            jax.ShapeDtypeStruct((TOK, FFW), bf16),
        ),
        in_specs=[smem, smem, hbm, hbm, hbm, hbm, hbm],
        out_specs=(hbm, hbm, hbm, vmem, vmem),
        scratch_shapes=[pltpu.VMEM(shape, t) for t in (f32, bf16, bf16, bf16, f32, bf16, bf16)]
        + [
            pltpu.SemaphoreType.DMA((4, CHUNKS)),
            pltpu.SemaphoreType.DMA((3, CHUNKS)),
            pltpu.SemaphoreType.DMA((REPLICAS,)),
        ],
        compiler_params=pltpu.CompilerParams(vmem_limit_bytes=52500 * 1024),
        name="adam_quantize",
    )(owner, slab, w, g, m, v, hidden)


ORDER = (0, 1, 7, 2, 6, 3, 5, 4)
LAGS = (1, 2, 3)


def deliver_kernel(mine, ordered, out, spread, same, cross, both, obuf, asem, ssem, rsem, lsem):
    r, s = lax.axis_index("replica"), lax.axis_index("shard")
    xh, y = r // 4, r % 4
    z, xl, c = s // 4, (s // 2) % 2, s % 2
    up, down, far = (y + 1) % 4, (y + 3) % 4, (y + 2) % 4
    role = (y + c) % 2
    partner = (y + 1 + 2 * role) % 4

    def owner_at(zz, cc):
        return zz * 4 + xl * 2 + cc

    exchange = [(i, dc) for i in range(ZS) for dc in range(2) if (ORDER[i], dc) != (0, 0)]
    to_up, to_down, to_far = ((xh * 4 + place, s) for place in (up, down, far))
    to_partner = (xh * 4 + partner, s)
    beside = z * 4 + (1 - xl) * 2 + c
    to_two, to_near, to_cross = ((1 - xh) * 4 + y, s), (r, beside), ((1 - xh) * 4 + y, beside)

    barrier = pltpu.get_barrier_semaphore()
    for i, dc in exchange:
        there = (r, owner_at((z + ORDER[i]) % ZS, (c + dc) % 2))
        pl.semaphore_signal(barrier, inc=1, device_id=there, device_id_type=MESH)
    for there in (to_up, to_down, to_far, to_two, to_near, to_cross):
        pl.semaphore_signal(barrier, inc=1, device_id=there, device_id_type=MESH)
    pl.semaphore_wait(barrier, len(exchange) + 6)

    pending = []
    serial = {}

    def send(key, src, dst, there):
        at = serial.setdefault(key, len(serial))
        copy = pltpu.make_async_remote_copy(
            src, dst, ssem.at[at], rsem.at[at], device_id=there, device_id_type=MESH
        )
        copy.start()
        pending.append(copy)

    def arrive(key, dst):
        at = serial[key]
        pltpu.make_async_remote_copy(
            dst, dst, ssem.at[at], rsem.at[at], device_id=(r, s), device_id_type=MESH
        ).wait_recv()

    own = pltpu.make_async_copy(mine.at[pl.ds(z * 4 + c * 2, 2)], spread.at[y, z, c], lsem.at[0])
    own.start()
    keep = pltpu.make_async_copy(ordered, both.at[pl.ds(0, TOK)], lsem.at[1])
    keep.start()
    theirs = both.at[pl.ds(TOK, TOK)]
    first = []
    for n, (i, dc) in enumerate(exchange):
        zz, cc = (z + ORDER[i]) % ZS, (c + dc) % 2
        copy = pltpu.make_async_remote_copy(
            mine.at[pl.ds(zz * 4 + cc * 2, 2)], spread.at[y, z, c], asem.at[0, n], asem.at[1, n],
            device_id=(r, owner_at(zz, cc)), device_id_type=MESH,
        )
        copy.start()
        first.append(copy)
        if n == 0:
            send("hidden", ordered, theirs, to_partner)

    def recv_slot(n):
        i, dc = exchange[n]
        return exchange.index((ORDER.index((ZS - ORDER[i]) % ZS), dc))

    def send_x(i, name, place):
        zz = (z + ORDER[i]) % ZS
        tile, other = spread.at[place, zz, role, 0], spread.at[place, zz, role, 1]
        send((i, name, "two"), tile, same.at[place, zz], to_two)
        send((i, name, "near"), other, cross.at[0, place, zz], to_near)
        send((i, name, "cross"), other, cross.at[1, place, zz], to_cross)

    def stage0(i):
        zz = (z + ORDER[i]) % ZS
        if i == 0:
            own.wait()
        for n, (k, dc) in enumerate(exchange):
            if k == i:
                got = spread.at[y, zz, (c + dc) % 2]
                pltpu.make_async_remote_copy(
                    got, got, asem.at[0, n], asem.at[1, recv_slot(n)], device_id=(r, s), device_id_type=MESH
                ).wait_recv()
        given, used = spread.at[y, zz, 1 - role], spread.at[y, zz, role]
        send_x(i, "own", y)
        send((i, "up"), given, given, to_up)
        send((i, "down"), given, given, to_down)
        send((i, "far"), used, used, to_far)

    def stage1(i):
        for name, place in (("up", down), ("down", up), ("far", far)):
            arrive((i, name), spread.at[place, (z + ORDER[i]) % ZS, role])
            send_x(i, name, place)

    def stage2(i):
        zz = (z + ORDER[i]) % ZS
        for name, place in (("own", y), ("up", down), ("down", up), ("far", far)):
            arrive((i, name, "two"), same.at[place, zz])
            arrive((i, name, "near"), cross.at[0, place, zz])
            arrive((i, name, "cross"), cross.at[1, place, zz])
        if i == 0:
            keep.wait()
            arrive("hidden", theirs)
        half = FFW // 2
        right = jnp.concatenate(
            [
                jnp.concatenate([spread[:, zz, role, 0].reshape(half, QB), same[:, zz].reshape(half, QB)], axis=0),
                cross[:, :, zz].reshape(FFW, QB),
            ],
            axis=1,
        )
        for whose in (1, 0):
            left = both[whose * TOK:(whose + 1) * TOK]
            value = jnp.dot(left, right, preferred_element_type=jnp.float32).astype(jnp.bfloat16)
            for k in range(2):
                part = value[:, k * QB:(k + 1) * QB]
                if whose:
                    obuf[i, k] = part
                else:
                    out[:, columns(i, k, role)] = part

    def columns(i, k, q):
        zz = (z + ORDER[i]) % ZS
        return pl.ds(pl.multiple_of((zz * 4 + ((xl + k) % 2) * 2 + q) * QB, QB), QB)

    def stage3(i):
        for k in range(2):
            send((i, "out", k), obuf.at[i, k], out.at[:, columns(i, k, role)], to_partner)

    stages = ((0, stage0), (LAGS[0], stage1), (LAGS[1], stage2), (LAGS[2], stage3))
    for t in range(ZS + LAGS[2]):
        for lag, stage in stages:
            if 0 <= t - lag < ZS:
                stage(t - lag)
    for i in range(ZS):
        for k in range(2):
            arrive((i, "out", k), out.at[:, columns(i, k, 1 - role)])
    for copy in first:
        copy.wait_send()
    for copy in pending:
        copy.wait_send()


def deliver(mine, ordered):
    copies = 17 * ZS + 1
    bf16 = jnp.bfloat16
    return pl.pallas_call(
        deliver_kernel,
        out_shape=jax.ShapeDtypeStruct((TOK, D), bf16),
        in_specs=[pl.BlockSpec(memory_space=pltpu.VMEM)] * 2,
        out_specs=pl.BlockSpec(memory_space=pltpu.VMEM),
        scratch_shapes=[
            pltpu.VMEM((4, ZS, 2, 2, QB, QB), bf16),
            pltpu.VMEM((4, ZS, QB, QB), bf16),
            pltpu.VMEM((2, 4, ZS, QB, QB), bf16),
            pltpu.VMEM((2 * TOK, FFW), bf16),
            pltpu.VMEM((ZS, 2, TOK, QB), bf16),
            pltpu.SemaphoreType.DMA((2, 2 * ZS - 1)),
            pltpu.SemaphoreType.DMA((copies,)),
            pltpu.SemaphoreType.DMA((copies,)),
            pltpu.SemaphoreType.DMA((2,)),
        ],
        compiler_params=pltpu.CompilerParams(
            collective_id=0, has_side_effects=True, vmem_limit_bytes=24 * 2**20
        ),
        name="deliver",
    )(mine, ordered)


def body(master_weight, gradient, first_moment, second_moment, hidden, owner_of_expert, slab_order):
    updated, moment_one, moment_two, outgoing, ordered = adam(
        owner_of_expert, slab_order, master_weight, gradient, first_moment, second_moment, hidden.reshape(TOK, FFW)
    )
    expert_out = deliver(outgoing, ordered)
    return updated, moment_one, moment_two, expert_out.reshape(1, 1, TOK, D)


def solution(mesh):
    learner = P(None, "replica", "shard")
    rollout = P("replica", "shard", None, None)
    return jax.shard_map(
        body,
        mesh=mesh,
        in_specs=(learner, learner, learner, learner, rollout, P(), P()),
        out_specs=(learner, learner, learner, rollout),
        check_vma=False,
    )
```

```python
import functools

import jax
import jax.numpy as jnp
from jax import lax
from jax.experimental import pallas as pl
from jax.experimental.pallas import tpu as pltpu
from jax.sharding import PartitionSpec as P

D = 4096
FFW = 1024
QB = 128
TOK = 384
EXPERTS = 32
REPLICAS = 8
ZS = 8

beta_one = 0.9
beta_two = 0.95
learn_rate = 0.004
adam_epsilon = 1e-08
step_count = 10.0
quant_limit = 448.0
scale_epsilon = 1e-06
first_fix = 1.0 - beta_one**step_count
second_fix = 1.0 - beta_two**step_count

MESH = pl.DeviceIdType.MESH
CHUNK = 4
CHUNKS = EXPERTS // CHUNK


def adam_kernel(
    owner, w_hbm, g_hbm, m_hbm, v_hbm, nw_hbm, nm_hbm, nv_hbm, mine,
    w_in, g_in, m_in, v_in, w_out, m_out, v_out, in_sem, out_sem,
):
    def loads(k):
        part = pl.ds(k * CHUNK, CHUNK)
        return [
            pltpu.make_async_copy(hbm.at[part], vmem.at[part], in_sem.at[j, k])
            for j, (hbm, vmem) in enumerate(((g_hbm, g_in), (m_hbm, m_in), (v_hbm, v_in), (w_hbm, w_in)))
        ]

    def stores(k):
        part = pl.ds(k * CHUNK, CHUNK)
        return [
            pltpu.make_async_copy(vmem.at[part], hbm.at[part], out_sem.at[j, k])
            for j, (vmem, hbm) in enumerate(((w_out, nw_hbm), (m_out, nm_hbm), (v_out, nv_hbm)))
        ]

    xl = (lax.axis_index("shard") // 2) % 2

    def place_of(e):
        to = owner[e]
        return (to // 4) * 4 + (to % 2) * 2 + (to // 2 + xl) % 2

    for k in range(CHUNKS):
        for copy in loads(k):
            copy.start()

    @pl.loop(0, CHUNKS)
    def _(k):
        for copy in loads(k):
            copy.wait()
        for i in range(CHUNK):
            e = k * CHUNK + i
            g = g_in[e].astype(jnp.float32)
            first = beta_one * m_in[e].astype(jnp.float32) + (1.0 - beta_one) * g
            second = beta_two * v_in[e].astype(jnp.float32) + (1.0 - beta_two) * g * g
            update = (learn_rate / first_fix) * first / (jnp.sqrt(second * (1.0 / second_fix)) + adam_epsilon)
            w = w_in[e] - update
            w_out[e] = w
            m_out[e] = first.astype(jnp.bfloat16)
            v_out[e] = second.astype(jnp.bfloat16)
            largest = jnp.max(jnp.abs(w), axis=(0, 1), keepdims=True)
            scale = ((largest + scale_epsilon) / quant_limit).astype(jnp.bfloat16).astype(jnp.float32)
            quantized = (w * (1.0 / scale)).astype(jnp.bfloat16).astype(jnp.float32)
            mine[place_of(e)] = (quantized * scale).astype(jnp.bfloat16)
        for copy in stores(k):
            copy.start()

    for k in range(CHUNKS):
        for copy in stores(k):
            copy.wait()


def adam(owner, w, g, m, v):
    shape = (EXPERTS, QB, QB)
    hbm = pl.BlockSpec(memory_space=pltpu.HBM)
    smem = pl.BlockSpec(memory_space=pltpu.SMEM)
    vmem = pl.BlockSpec(memory_space=pltpu.VMEM)
    f32, bf16 = jnp.float32, jnp.bfloat16
    return pl.pallas_call(
        adam_kernel,
        out_shape=(
            jax.ShapeDtypeStruct(shape, f32),
            jax.ShapeDtypeStruct(shape, bf16),
            jax.ShapeDtypeStruct(shape, bf16),
            jax.ShapeDtypeStruct(shape, bf16),
        ),
        in_specs=[smem, hbm, hbm, hbm, hbm],
        out_specs=(hbm, hbm, hbm, vmem),
        scratch_shapes=[pltpu.VMEM(shape, t) for t in (f32, bf16, bf16, bf16, f32, bf16, bf16)]
        + [
            pltpu.SemaphoreType.DMA((4, CHUNKS)),
            pltpu.SemaphoreType.DMA((3, CHUNKS)),
        ],
        compiler_params=pltpu.CompilerParams(vmem_limit_bytes=53400 * 1024),
        name="adam_quantize",
    )(owner, w, g, m, v)


ORDER = (0, 1, 7, 2, 6, 3, 5, 4)
LAGS = (2, 5, 6)
SWAP = 2
FIRST_X = (1, 3, 5)


def deliver_kernel(
    slab, mine, hidden, out, spread, same, cross, passing, held, theirs, both, obuf, asem, ssem, rsem, lsem
):
    r, s = lax.axis_index("replica"), lax.axis_index("shard")
    xh, y = r // 4, r % 4
    z, xl, c = s // 4, (s // 2) % 2, s % 2
    up, down, far = (y + 1) % 4, (y + 3) % 4, (y + 2) % 4
    role = (y + c) % 2
    partner = (y + 1 + 2 * role) % 4

    def owner_at(zz, cc):
        return zz * 4 + xl * 2 + cc

    exchange = [(i, dc) for i in range(ZS) for dc in range(2) if (ORDER[i], dc) != (0, 0)]
    to_up, to_down, to_far = ((xh * 4 + place, s) for place in (up, down, far))
    to_partner = (xh * 4 + partner, s)
    beside = z * 4 + (1 - xl) * 2 + c
    to_two, to_near, to_cross = ((1 - xh) * 4 + y, s), (r, beside), ((1 - xh) * 4 + y, beside)

    barrier = pltpu.get_barrier_semaphore()
    for i, dc in exchange:
        there = (r, owner_at((z + ORDER[i]) % ZS, (c + dc) % 2))
        pl.semaphore_signal(barrier, inc=1, device_id=there, device_id_type=MESH)
    for there in (to_up, to_down, to_far, to_two, to_near, to_cross):
        pl.semaphore_signal(barrier, inc=1, device_id=there, device_id_type=MESH)
    pl.semaphore_wait(barrier, len(exchange) + 6)

    pending = []
    serial = {}

    def send(key, src, dst, there):
        at = serial.setdefault(key, len(serial))
        copy = pltpu.make_async_remote_copy(
            src, dst, ssem.at[at], rsem.at[at], device_id=there, device_id_type=MESH
        )
        copy.start()
        pending.append(copy)

    def arrive(key, dst):
        at = serial[key]
        pltpu.make_async_remote_copy(
            dst, dst, ssem.at[at], rsem.at[at], device_id=(r, s), device_id_type=MESH
        ).wait_recv()

    own = pltpu.make_async_copy(mine.at[pl.ds(z * 4 + c * 2, 2)], spread.at[y, z, c], lsem.at[0])
    own.start()
    keep = []
    for j in range(REPLICAS):
        keep.append(pltpu.make_async_copy(hidden.at[:, pl.ds(j * QB, QB)], held.at[j], lsem.at[1 + j]))
        keep[j].start()
    first = []
    for n, (i, dc) in enumerate(exchange):
        zz, cc = (z + ORDER[i]) % ZS, (c + dc) % 2
        copy = pltpu.make_async_remote_copy(
            mine.at[pl.ds(zz * 4 + cc * 2, 2)], spread.at[y, z, c], asem.at[0, n], asem.at[1, n],
            device_id=(r, owner_at(zz, cc)), device_id_type=MESH,
        )
        copy.start()
        first.append(copy)

    def recv_slot(n):
        i, dc = exchange[n]
        return exchange.index((ORDER.index((ZS - ORDER[i]) % ZS), dc))

    def send_x(i, name, place):
        zz = (z + ORDER[i]) % ZS
        tile, other = spread.at[place, zz, role, 0], spread.at[place, zz, role, 1]
        send((i, name, "two"), tile, same.at[place, zz], to_two)
        if i in FIRST_X and name != "own":
            return
        send((i, name, "near"), other, cross.at[0, place, zz], to_near)
        send((i, name, "cross"), other, cross.at[1, place, zz], to_cross)

    def stage0(i):
        zz = (z + ORDER[i]) % ZS
        if i == 0:
            own.wait()
        for n, (k, dc) in enumerate(exchange):
            if k == i:
                got = spread.at[y, zz, (c + dc) % 2]
                pltpu.make_async_remote_copy(
                    got, got, asem.at[0, n], asem.at[1, recv_slot(n)], device_id=(r, s), device_id_type=MESH
                ).wait_recv()
        given, used = spread.at[y, zz, 1 - role], spread.at[y, zz, role]
        send_x(i, "own", y)
        if i in FIRST_X:
            given, used = spread.at[y, zz, 1 - role, 0], spread.at[y, zz, role, 0]
            other = spread.at[y, zz, 1 - role, 1]
            for side, there in enumerate((to_near, to_cross)):
                send((i, "pass", side), other, passing.at[side, FIRST_X.index(i)], there)
        send((i, "up"), given, given, to_up)
        send((i, "down"), given, given, to_down)
        send((i, "far"), used, used, to_far)

    def stage1(i):
        zz = (z + ORDER[i]) % ZS
        for name, place in (("up", down), ("down", up), ("far", far)):
            got = spread.at[place, zz, role, 0] if i in FIRST_X else spread.at[place, zz, role]
            arrive((i, name), got)
            send_x(i, name, place)
        if i in FIRST_X:
            for side, name in enumerate(("near", "cross")):
                used, other = cross.at[side, y, zz], passing.at[side, FIRST_X.index(i)]
                arrive((i, "own", name), used)
                send((i, "far", side), used, used, to_far)
                arrive((i, "pass", side), other)
                send((i, "up", side), other, used, to_up)
                send((i, "down", side), other, used, to_down)

    def stage2(i):
        zz = (z + ORDER[i]) % ZS
        for name, place in (("own", y), ("up", down), ("down", up), ("far", far)):
            arrive((i, name, "two"), same.at[place, zz])
            if i not in FIRST_X:
                arrive((i, name, "near"), cross.at[0, place, zz])
                arrive((i, name, "cross"), cross.at[1, place, zz])
            elif name != "own":
                for side in range(2):
                    arrive((i, name, side), cross.at[side, place, zz])
        if i == 0:
            for j in range(REPLICAS):
                arrive(("slab", j), theirs.at[j])
            for whose, slabs in enumerate((held, theirs)):
                for j in range(REPLICAS):
                    both[whose * TOK:(whose + 1) * TOK, j * QB:(j + 1) * QB] = slabs[slab[(xh * 4 + j) % REPLICAS]]
        half = FFW // 2
        right = jnp.concatenate(
            [
                jnp.concatenate([spread[:, zz, role, 0].reshape(half, QB), same[:, zz].reshape(half, QB)], axis=0),
                cross[:, :, zz].reshape(FFW, QB),
            ],
            axis=1,
        )
        for whose in (1, 0):
            left = both[whose * TOK:(whose + 1) * TOK]
            value = jnp.dot(left, right, preferred_element_type=jnp.float32).astype(jnp.bfloat16)
            for k in range(2):
                part = value[:, k * QB:(k + 1) * QB]
                if whose:
                    obuf[i, k] = part
                else:
                    out[:, columns(i, k, role)] = part

    def columns(i, k, q):
        zz = (z + ORDER[i]) % ZS
        return pl.ds(pl.multiple_of((zz * 4 + ((xl + k) % 2) * 2 + q) * QB, QB), QB)

    def stage3(i):
        for k in range(2):
            send((i, "out", k), obuf.at[i, k], out.at[:, columns(i, k, role)], to_partner)

    def swap_slabs(t):
        for j in range(t * SWAP, (t + 1) * SWAP):
            keep[j].wait()
            send(("slab", j), held.at[j], theirs.at[j], to_partner)

    stages = ((0, stage0), (LAGS[0], stage1), (LAGS[1], stage2), (LAGS[2], stage3))
    for t in range(ZS + LAGS[2]):
        for lag, stage in stages:
            if 0 <= t - lag < ZS:
                stage(t - lag)
            if stage is stage1 and t * SWAP < REPLICAS:
                swap_slabs(t)
    for i in range(ZS):
        for k in range(2):
            arrive((i, "out", k), out.at[:, columns(i, k, 1 - role)])
    for copy in first:
        copy.wait_send()
    for copy in pending:
        copy.wait_send()


def deliver(slab, mine, hidden):
    copies = 20 * ZS
    bf16 = jnp.bfloat16
    return pl.pallas_call(
        deliver_kernel,
        out_shape=jax.ShapeDtypeStruct((TOK, D), bf16),
        in_specs=[
            pl.BlockSpec(memory_space=pltpu.SMEM),
            pl.BlockSpec(memory_space=pltpu.VMEM),
            pl.BlockSpec(memory_space=pl.ANY),
        ],
        out_specs=pl.BlockSpec(memory_space=pltpu.VMEM),
        scratch_shapes=[
            pltpu.VMEM((4, ZS, 2, 2, QB, QB), bf16),
            pltpu.VMEM((4, ZS, QB, QB), bf16),
            pltpu.VMEM((2, 4, ZS, QB, QB), bf16),
            pltpu.VMEM((2, max(len(FIRST_X), 1), QB, QB), bf16),
            pltpu.VMEM((REPLICAS, TOK, QB), bf16),
            pltpu.VMEM((REPLICAS, TOK, QB), bf16),
            pltpu.VMEM((2 * TOK, FFW), bf16),
            pltpu.VMEM((ZS, 2, TOK, QB), bf16),
            pltpu.SemaphoreType.DMA((2, 2 * ZS - 1)),
            pltpu.SemaphoreType.DMA((copies,)),
            pltpu.SemaphoreType.DMA((copies,)),
            pltpu.SemaphoreType.DMA((1 + REPLICAS,)),
        ],
        compiler_params=pltpu.CompilerParams(
            collective_id=0, has_side_effects=True, vmem_limit_bytes=24 * 2**20
        ),
        name="deliver",
    )(slab, mine, hidden)


def body(master_weight, gradient, first_moment, second_moment, hidden, owner_of_expert, slab_order):
    updated, moment_one, moment_two, outgoing = adam(
        owner_of_expert, master_weight, gradient, first_moment, second_moment
    )
    expert_out = deliver(slab_order, outgoing, hidden.reshape(TOK, FFW))
    return updated, moment_one, moment_two, expert_out.reshape(1, 1, TOK, D)


def solution(mesh):
    learner = P(None, "replica", "shard")
    rollout = P("replica", "shard", None, None)
    return jax.shard_map(
        body,
        mesh=mesh,
        in_specs=(learner, learner, learner, learner, rollout, P(), P()),
        out_specs=(learner, learner, learner, rollout),
        check_vma=False,
    )
```

```python
import functools

import jax
import jax.numpy as jnp
from jax import lax
from jax.experimental import pallas as pl
from jax.experimental.pallas import tpu as pltpu
from jax.sharding import PartitionSpec as P

D = 4096
FFW = 1024
QB = 128
TOK = 384
EXPERTS = 32
REPLICAS = 8
ZS = 8

beta_one = 0.9
beta_two = 0.95
learn_rate = 0.004
adam_epsilon = 1e-08
step_count = 10.0
quant_limit = 448.0
scale_epsilon = 1e-06
first_fix = 1.0 - beta_one**step_count
second_fix = 1.0 - beta_two**step_count

MESH = pl.DeviceIdType.MESH
CHUNK = 8
CHUNKS = EXPERTS // CHUNK


def adam_kernel(
    owner, w_hbm, g_hbm, m_hbm, v_hbm, nw_hbm, nm_hbm, nv_hbm, mine,
    w_in, g_in, m_in, v_in, w_out, m_out, v_out, in_sem, out_sem,
):
    def loads(k):
        part = pl.ds(k * CHUNK, CHUNK)
        return [
            pltpu.make_async_copy(hbm.at[part], vmem.at[part], in_sem.at[j, k])
            for j, (hbm, vmem) in enumerate(((g_hbm, g_in), (m_hbm, m_in), (v_hbm, v_in), (w_hbm, w_in)))
        ]

    def stores(k):
        part = pl.ds(k * CHUNK, CHUNK)
        return [
            pltpu.make_async_copy(vmem.at[part], hbm.at[part], out_sem.at[j, k])
            for j, (vmem, hbm) in enumerate(((w_out, nw_hbm), (m_out, nm_hbm), (v_out, nv_hbm)))
        ]

    xl = (lax.axis_index("shard") // 2) % 2

    def place_of(e):
        to = owner[e]
        return (to // 4) * 4 + (to % 2) * 2 + (to // 2 + xl) % 2

    for k in range(CHUNKS):
        for copy in loads(k):
            copy.start()

    @pl.loop(0, CHUNKS)
    def _(k):
        for copy in loads(k):
            copy.wait()
        for i in range(CHUNK):
            e = k * CHUNK + i
            g = g_in[e].astype(jnp.float32)
            first = beta_one * m_in[e].astype(jnp.float32) + (1.0 - beta_one) * g
            second = beta_two * v_in[e].astype(jnp.float32) + (1.0 - beta_two) * g * g
            update = (learn_rate / first_fix) * first / (jnp.sqrt(second * (1.0 / second_fix)) + adam_epsilon)
            w = w_in[e] - update
            w_out[e] = w
            m_out[e] = first.astype(jnp.bfloat16)
            v_out[e] = second.astype(jnp.bfloat16)
            largest = jnp.max(jnp.abs(w), axis=(0, 1), keepdims=True)
            scale = ((largest + scale_epsilon) / quant_limit).astype(jnp.bfloat16).astype(jnp.float32)
            quantized = (w * (1.0 / scale)).astype(jnp.bfloat16).astype(jnp.float32)
            mine[place_of(e)] = (quantized * scale).astype(jnp.bfloat16)
        for copy in stores(k):
            copy.start()

    for k in range(CHUNKS):
        for copy in stores(k):
            copy.wait()


def adam(owner, w, g, m, v):
    shape = (EXPERTS, QB, QB)
    hbm = pl.BlockSpec(memory_space=pltpu.HBM)
    smem = pl.BlockSpec(memory_space=pltpu.SMEM)
    vmem = pl.BlockSpec(memory_space=pltpu.VMEM)
    f32, bf16 = jnp.float32, jnp.bfloat16
    return pl.pallas_call(
        adam_kernel,
        out_shape=(
            jax.ShapeDtypeStruct(shape, f32),
            jax.ShapeDtypeStruct(shape, bf16),
            jax.ShapeDtypeStruct(shape, bf16),
            jax.ShapeDtypeStruct(shape, bf16),
        ),
        in_specs=[smem, hbm, hbm, hbm, hbm],
        out_specs=(hbm, hbm, hbm, vmem),
        scratch_shapes=[pltpu.VMEM(shape, t) for t in (f32, bf16, bf16, bf16, f32, bf16, bf16)]
        + [
            pltpu.SemaphoreType.DMA((4, CHUNKS)),
            pltpu.SemaphoreType.DMA((3, CHUNKS)),
        ],
        compiler_params=pltpu.CompilerParams(vmem_limit_bytes=53400 * 1024),
        name="adam_quantize",
    )(owner, w, g, m, v)


ORDER = (0, 1, 7, 2, 6, 3, 5, 4)
LAGS = (2, 5, 6)
SWAP = 2
FIRST_X = (1, 3, 5)


def deliver_kernel(
    slab, mine, hidden, out, spread, same, cross, passing, held, theirs, both, obuf, asem, ssem, rsem, lsem
):
    r, s = lax.axis_index("replica"), lax.axis_index("shard")
    xh, y = r // 4, r % 4
    z, xl, c = s // 4, (s // 2) % 2, s % 2
    up, down, far = (y + 1) % 4, (y + 3) % 4, (y + 2) % 4
    role = (y + c) % 2
    partner = (y + 1 + 2 * role) % 4

    def owner_at(zz, cc):
        return zz * 4 + xl * 2 + cc

    exchange = [(i, dc) for i in range(ZS) for dc in range(2) if (ORDER[i], dc) != (0, 0)]
    to_up, to_down, to_far = ((xh * 4 + place, s) for place in (up, down, far))
    to_partner = (xh * 4 + partner, s)
    beside = z * 4 + (1 - xl) * 2 + c
    to_two, to_near, to_cross = ((1 - xh) * 4 + y, s), (r, beside), ((1 - xh) * 4 + y, beside)

    barrier = pltpu.get_barrier_semaphore()
    for i, dc in exchange:
        there = (r, owner_at((z + ORDER[i]) % ZS, (c + dc) % 2))
        pl.semaphore_signal(barrier, inc=1, device_id=there, device_id_type=MESH)
    for there in (to_up, to_down, to_far, to_two, to_near, to_cross):
        pl.semaphore_signal(barrier, inc=1, device_id=there, device_id_type=MESH)
    pl.semaphore_wait(barrier, len(exchange) + 6)

    pending = []
    serial = {}

    def send(key, src, dst, there):
        at = serial.setdefault(key, len(serial))
        copy = pltpu.make_async_remote_copy(
            src, dst, ssem.at[at], rsem.at[at], device_id=there, device_id_type=MESH
        )
        copy.start()
        pending.append(copy)

    def arrive(key, dst):
        at = serial[key]
        pltpu.make_async_remote_copy(
            dst, dst, ssem.at[at], rsem.at[at], device_id=(r, s), device_id_type=MESH
        ).wait_recv()

    own = pltpu.make_async_copy(mine.at[pl.ds(z * 4 + c * 2, 2)], spread.at[y, z, c], lsem.at[0])
    own.start()
    keep = []
    for j in range(REPLICAS):
        keep.append(pltpu.make_async_copy(hidden.at[:, pl.ds(j * QB, QB)], held.at[j], lsem.at[1 + j]))
        keep[j].start()
    first = []
    for n, (i, dc) in enumerate(exchange):
        zz, cc = (z + ORDER[i]) % ZS, (c + dc) % 2
        copy = pltpu.make_async_remote_copy(
            mine.at[pl.ds(zz * 4 + cc * 2, 2)], spread.at[y, z, c], asem.at[0, n], asem.at[1, n],
            device_id=(r, owner_at(zz, cc)), device_id_type=MESH,
        )
        copy.start()
        first.append(copy)

    def recv_slot(n):
        i, dc = exchange[n]
        return exchange.index((ORDER.index((ZS - ORDER[i]) % ZS), dc))

    def send_x(i, name, place):
        zz = (z + ORDER[i]) % ZS
        tile, other = spread.at[place, zz, role, 0], spread.at[place, zz, role, 1]
        send((i, name, "two"), tile, same.at[place, zz], to_two)
        if i in FIRST_X and name != "own":
            return
        send((i, name, "near"), other, cross.at[0, place, zz], to_near)
        send((i, name, "cross"), other, cross.at[1, place, zz], to_cross)

    def stage0(i):
        zz = (z + ORDER[i]) % ZS
        if i == 0:
            own.wait()
        for n, (k, dc) in enumerate(exchange):
            if k == i:
                got = spread.at[y, zz, (c + dc) % 2]
                pltpu.make_async_remote_copy(
                    got, got, asem.at[0, n], asem.at[1, recv_slot(n)], device_id=(r, s), device_id_type=MESH
                ).wait_recv()
        given, used = spread.at[y, zz, 1 - role], spread.at[y, zz, role]
        send_x(i, "own", y)
        if i in FIRST_X:
            given, used = spread.at[y, zz, 1 - role, 0], spread.at[y, zz, role, 0]
            other = spread.at[y, zz, 1 - role, 1]
            for side, there in enumerate((to_near, to_cross)):
                send((i, "pass", side), other, passing.at[side, FIRST_X.index(i)], there)
        send((i, "up"), given, given, to_up)
        send((i, "down"), given, given, to_down)
        send((i, "far"), used, used, to_far)

    def stage1(i):
        zz = (z + ORDER[i]) % ZS
        for name, place in (("up", down), ("down", up), ("far", far)):
            got = spread.at[place, zz, role, 0] if i in FIRST_X else spread.at[place, zz, role]
            arrive((i, name), got)
            send_x(i, name, place)
        if i in FIRST_X:
            for side, name in enumerate(("near", "cross")):
                used, other = cross.at[side, y, zz], passing.at[side, FIRST_X.index(i)]
                arrive((i, "own", name), used)
                send((i, "far", side), used, used, to_far)
                arrive((i, "pass", side), other)
                send((i, "up", side), other, used, to_up)
                send((i, "down", side), other, used, to_down)

    def stage2(i):
        zz = (z + ORDER[i]) % ZS
        for name, place in (("own", y), ("up", down), ("down", up), ("far", far)):
            arrive((i, name, "two"), same.at[place, zz])
            if i not in FIRST_X:
                arrive((i, name, "near"), cross.at[0, place, zz])
                arrive((i, name, "cross"), cross.at[1, place, zz])
            elif name != "own":
                for side in range(2):
                    arrive((i, name, side), cross.at[side, place, zz])
        if i == 0:
            for j in range(REPLICAS):
                arrive(("slab", j), theirs.at[j])
            for whose, slabs in enumerate((held, theirs)):
                for j in range(REPLICAS):
                    both[whose * TOK:(whose + 1) * TOK, j * QB:(j + 1) * QB] = slabs[slab[(xh * 4 + j) % REPLICAS]]
        half = FFW // 2
        right = jnp.concatenate(
            [
                jnp.concatenate([spread[:, zz, role, 0].reshape(half, QB), same[:, zz].reshape(half, QB)], axis=0),
                cross[:, :, zz].reshape(FFW, QB),
            ],
            axis=1,
        )
        for whose in (1, 0):
            left = both[whose * TOK:(whose + 1) * TOK]
            value = jnp.dot(left, right, preferred_element_type=jnp.float32).astype(jnp.bfloat16)
            for k in range(2):
                part = value[:, k * QB:(k + 1) * QB]
                if whose:
                    obuf[i, k] = part
                else:
                    out[:, columns(i, k, role)] = part

    def columns(i, k, q):
        zz = (z + ORDER[i]) % ZS
        return pl.ds(pl.multiple_of((zz * 4 + ((xl + k) % 2) * 2 + q) * QB, QB), QB)

    def stage3(i):
        for k in range(2):
            send((i, "out", k), obuf.at[i, k], out.at[:, columns(i, k, role)], to_partner)

    def swap_slabs(t):
        for j in range(t * SWAP, (t + 1) * SWAP):
            keep[j].wait()
            send(("slab", j), held.at[j], theirs.at[j], to_partner)

    stages = ((0, stage0), (LAGS[0], stage1), (LAGS[1], stage2), (LAGS[2], stage3))
    for t in range(ZS + LAGS[2]):
        for lag, stage in stages:
            if 0 <= t - lag < ZS:
                stage(t - lag)
            if stage is stage1 and t * SWAP < REPLICAS:
                swap_slabs(t)
    for i in range(ZS):
        for k in range(2):
            arrive((i, "out", k), out.at[:, columns(i, k, 1 - role)])
    for copy in first:
        copy.wait_send()
    for copy in pending:
        copy.wait_send()


def deliver(slab, mine, hidden):
    copies = 20 * ZS
    bf16 = jnp.bfloat16
    return pl.pallas_call(
        deliver_kernel,
        out_shape=jax.ShapeDtypeStruct((TOK, D), bf16),
        in_specs=[
            pl.BlockSpec(memory_space=pltpu.SMEM),
            pl.BlockSpec(memory_space=pltpu.VMEM),
            pl.BlockSpec(memory_space=pl.ANY),
        ],
        out_specs=pl.BlockSpec(memory_space=pltpu.VMEM),
        scratch_shapes=[
            pltpu.VMEM((4, ZS, 2, 2, QB, QB), bf16),
            pltpu.VMEM((4, ZS, QB, QB), bf16),
            pltpu.VMEM((2, 4, ZS, QB, QB), bf16),
            pltpu.VMEM((2, max(len(FIRST_X), 1), QB, QB), bf16),
            pltpu.VMEM((REPLICAS, TOK, QB), bf16),
            pltpu.VMEM((REPLICAS, TOK, QB), bf16),
            pltpu.VMEM((2 * TOK, FFW), bf16),
            pltpu.VMEM((ZS, 2, TOK, QB), bf16),
            pltpu.SemaphoreType.DMA((2, 2 * ZS - 1)),
            pltpu.SemaphoreType.DMA((copies,)),
            pltpu.SemaphoreType.DMA((copies,)),
            pltpu.SemaphoreType.DMA((1 + REPLICAS,)),
        ],
        compiler_params=pltpu.CompilerParams(
            collective_id=0, has_side_effects=True, vmem_limit_bytes=24 * 2**20
        ),
        name="deliver",
    )(slab, mine, hidden)


def body(master_weight, gradient, first_moment, second_moment, hidden, owner_of_expert, slab_order):
    updated, moment_one, moment_two, outgoing = adam(
        owner_of_expert, master_weight, gradient, first_moment, second_moment
    )
    expert_out = deliver(slab_order, outgoing, hidden.reshape(TOK, FFW))
    return updated, moment_one, moment_two, expert_out.reshape(1, 1, TOK, D)


def solution(mesh):
    learner = P(None, "replica", "shard")
    rollout = P("replica", "shard", None, None)
    return jax.shard_map(
        body,
        mesh=mesh,
        in_specs=(learner, learner, learner, learner, rollout, P(), P()),
        out_specs=(learner, learner, learner, rollout),
        check_vma=False,
    )
```
